32 devices in a mesh: groups: 2 (over x), expert: 4 (over y, core), dp: 4 (over z).
Axes of the slice: x: 2, y: 2, z: 4, core: 2. Of those that a mesh axis runs over, the one named last changes fastest.
Arguments:
- tokens: bfloat16 [4096, 7168], P(('groups', 'expert', 'dp')), parts along dimension 0, may hold values from -6 to 6
- cotangent: bfloat16 [4096, 7168], P(('groups', 'expert', 'dp')), parts along dimension 0, may hold values from -1.1953125 to 1.1953125
- route_ids: int32 [4096, 8], P(('groups', 'expert', 'dp')), parts along dimension 0, may hold values from 0 to 255, as said below
- route_weight: bfloat16 [4096, 8], P(('groups', 'expert', 'dp')), parts along dimension 0, may hold values from 0.049804688 to 0.5
- gate_weight: bfloat16 [4, 7168, 1024], P('expert', None, 'dp'), may hold values from -0.0625 to 0.0625
- up_weight: bfloat16 [4, 7168, 1024], P('expert', None, 'dp'), may hold values from -0.0625 to 0.0625
- down_weight: bfloat16 [4, 1024, 7168], P('expert', 'dp'), may hold values from -0.0625 to 0.0625
Outputs:
- grad_gate: bfloat16 [8, 7168, 1024], P(('groups', 'expert'), None, 'dp'), parts along dimension 0
- grad_up: bfloat16 [8, 7168, 1024], P(('groups', 'expert'), None, 'dp'), parts along dimension 0
- route_grad: float32 [4096, 8], P(('groups', 'expert', 'dp')), parts along dimension 0
The draws below stay inside these ranges and needn't reach their ends.
There are 2 independent parts, one for each index of `groups`. The reference program is written for one: setup_inputs(seed, part) draws one part's arguments, and reference() takes and returns one part's arrays. A program takes and returns all parts, laid end to end along the dimension named above; an argument that names none is the same for every part. Nothing has to cross between parts.
Inputs may be any that keep to these rules, and one draw needn't show every extreme that they name: `route_ids`: each token names 8 different experts. Of the tokens of one device (aligned blocks of 128 rows), at most 8 name any one expert below 4, and one such expert is named by exactly 8 tokens of every device.
All inputs are finite; a program needn't handle non-finite values.
Results may differ from the reference program's by a relative error of at most 0.0049.
Values may be sent and summed in bfloat16 or wider, within the bound.
No kernel may reach another device: no remote copies, remote signals or barrier semaphores. Data moves between devices by JAX's collectives and lax.ppermute only.
A program may use at most 128 MiB of HBM per device.

```python
import math
import jax
import jax.numpy as jnp
from jax import lax

D = 7168
FF = 1024
ALL_EXPERTS = 256
TOPK = 8
TOK_DEV = 128
EXPERTS = 4
CAP = 8
TOKENS = 2048
N_DP = 4


def draw_route_ids(key, part):
    id_span = ALL_EXPERTS // TOPK
    blocks = TOKENS // TOK_DEV
    key_list = jax.random.split(key, 5)
    hot_id = jax.random.randint(key_list[0], (), 0, EXPERTS)
    offsets = jax.random.randint(key_list[1], (blocks, 1), 0, id_span - 1)
    column = jnp.arange(TOK_DEV, dtype=jnp.int32)[None, :]
    others = (offsets + column) % (id_span - 1)
    others = jnp.where(others >= hot_id, others + 1, others)
    lead_ids = jnp.where(column < CAP, hot_id, others)
    shuffles = jax.vmap(lambda sub_key: jax.random.permutation(sub_key, TOK_DEV))(jax.random.split(key_list[2], blocks))
    lead_ids = jnp.take_along_axis(lead_ids, shuffles, axis=1).reshape(TOKENS)
    tail_ids = jax.random.randint(key_list[3], (TOKENS, TOPK - 1), 0, id_span) + id_span * jnp.arange(1, TOPK, dtype=jnp.int32)[None, :]
    chosen = jnp.concatenate([lead_ids[:, None], tail_ids], axis=1)
    orders = jax.vmap(lambda sub_key: jax.random.permutation(sub_key, TOPK))(jax.random.split(key_list[4], TOKENS))
    return jnp.take_along_axis(chosen, orders, axis=1).astype(jnp.int32)


def block_scale(key, extent, pieces, least, high):
    gain, own = 1.0, jax.random.fold_in(key, 6)
    for dim, parts in pieces:
        steps = jnp.exp(jax.random.uniform(jax.random.fold_in(own, dim), (parts,), jnp.float32, least / len(pieces), high / len(pieces)))
        gain = gain * jnp.repeat(steps, extent[dim] // parts).reshape([-1 if axis == dim else 1 for axis in range(len(extent))])
    return gain


def normal_values(own_key, extent, scale, most, shards=(), kind=jnp.bfloat16):
    result = jax.random.normal(own_key, extent, jnp.float32) * scale
    if len(shards) > 0:
        result = block_scale(own_key, extent, shards, -0.22, 0.18) * result
    return jnp.clip(result, min=-most, max=most).astype(kind)


def setup_inputs(seed: int = 0, part: int = 0) -> dict:
    key_of = jax.random.split(jax.random.key(seed), 8)
    own_keys = jax.random.split(jax.random.fold_in(key_of[7], part), 8)
    tokens = normal_values(own_keys[0], (TOKENS, D), 1.0, 6.0, ((0, 16),))
    cotangent = normal_values(own_keys[1], (TOKENS, D), 0.2, 1.1953125, ((0, 16),))
    route_ids = draw_route_ids(jax.random.fold_in(jax.random.fold_in(key_of[7], part), 71), part)
    route_weight = jnp.clip(jnp.exp(math.log(0.5) - 2.306499 * jax.random.uniform(own_keys[3], (TOKENS, TOPK), jnp.float32) ** block_scale(own_keys[3], (TOKENS, TOPK), ((0, 16),), -0.2, 0.2)), 0.049804688, 0.5).astype(jnp.bfloat16)
    gate_weight = normal_values(key_of[4], (EXPERTS, D, FF), D ** -0.5, 0.0625, ((0, 4), (2, 4)))
    up_weight = normal_values(key_of[5], (EXPERTS, D, FF), D ** -0.5, 0.0625, ((0, 4), (2, 4)))
    down_weight = normal_values(key_of[6], (EXPERTS, FF, D), D ** -0.5, 0.0625, ((0, 4), (1, 4)))
    return {"tokens": tokens, "cotangent": cotangent, "route_ids": route_ids, "route_weight": route_weight, "gate_weight": gate_weight, "up_weight": up_weight, "down_weight": down_weight}


def reference(tokens, cotangent, route_ids, route_weight, gate_weight, up_weight, down_weight):
    most_rows = EXPERTS * N_DP * CAP

    def one_expert(expert_id):
        chosen = route_ids == expert_id
        picked = jnp.any(chosen, axis=1)
        weight_tok = jnp.sum(jnp.where(chosen, route_weight.astype(jnp.float32), 0.0), axis=1)
        row_order = jnp.argsort(jnp.where(picked, 0, 1).astype(jnp.int32), stable=True)[:most_rows]
        live_rows = picked[row_order].astype(jnp.float32)
        row_block = tokens[row_order]
        cot_block = cotangent[row_order]
        gate_pre = jnp.dot(row_block, gate_weight[expert_id], preferred_element_type=jnp.float32)
        up_pre = jnp.dot(row_block, up_weight[expert_id], preferred_element_type=jnp.float32)
        back_proj = jnp.dot(cot_block, down_weight[expert_id].T, preferred_element_type=jnp.float32)
        gate_sig = jax.nn.sigmoid(gate_pre)
        gate_act = gate_pre * gate_sig
        slot_sum = jnp.sum(gate_act * up_pre * back_proj, axis=1) * live_rows
        act_grad = (weight_tok[row_order] * live_rows)[:, None] * back_proj
        d_gate = (act_grad * up_pre * gate_sig * (1.0 + gate_pre * (1.0 - gate_sig))).astype(jnp.bfloat16)
        d_up = (act_grad * gate_act).astype(jnp.bfloat16)
        grad_g = jnp.dot(row_block.T, d_gate, preferred_element_type=jnp.float32).astype(jnp.bfloat16)
        grad_u = jnp.dot(row_block.T, d_up, preferred_element_type=jnp.float32).astype(jnp.bfloat16)
        tok_sum = jnp.zeros((TOKENS,), jnp.float32).at[row_order].add(slot_sum)
        slot_grad = jnp.where(chosen, tok_sum[:, None], jnp.zeros((), jnp.float32))
        return grad_g, grad_u, slot_grad

    grad_gate, grad_up, slot_grads = lax.map(one_expert, jnp.arange(EXPERTS, dtype=jnp.int32))
    return grad_gate, grad_up, jnp.sum(slot_grads, axis=0)
```

```python
import functools
import jax
import jax.numpy as jnp
from jax import lax
from jax.experimental import pallas as pl
from jax.experimental.pallas import tpu as pltpu
from jax.sharding import PartitionSpec as P

CAP = 8
LANES = 128


def pick_kernel(experts, steps, me_ref, ids_ref, weight_ref, tok_ref, cot_ref, *refs):
    row_refs, rank_ref, onehot_ref = refs[:-2], refs[-2], refs[-1]
    step = pl.program_id(0)
    count = experts * CAP
    tok_count, width = tok_ref.shape
    me = me_ref[0]
    total = width * steps

    @pl.when(step == 0)
    def _():
        ids = ids_ref[...]
        weight = weight_ref[...].astype(jnp.float32)
        expert_row = lax.broadcasted_iota(jnp.int32, (experts, tok_count), 0)
        named = jnp.zeros((experts, tok_count), jnp.float32)
        named_xor = jnp.zeros((experts, tok_count), jnp.float32)
        weight_xor = jnp.zeros((experts, tok_count), jnp.float32)
        for route in range(ids.shape[0]):
            own = jnp.broadcast_to(ids[route : route + 1], (experts, tok_count))
            hit = own == expert_row
            hit_xor = own == (expert_row ^ me)
            named = named + hit.astype(jnp.float32)
            named_xor = named_xor + hit_xor.astype(jnp.float32)
            weight_xor = weight_xor + jnp.where(hit_xor, weight[route : route + 1], 0.0)
        earlier = (
            lax.broadcasted_iota(jnp.int32, (tok_count, tok_count), 0)
            < lax.broadcasted_iota(jnp.int32, (tok_count, tok_count), 1)
        ).astype(jnp.bfloat16)
        both = jnp.concatenate([named, named_xor], axis=0).astype(jnp.bfloat16)
        ranks = jnp.dot(both, earlier, preferred_element_type=jnp.float32)
        rank_ref[...] = jnp.where(named > 0.0, ranks[:experts], -1.0)
        rank_xor = jnp.where(named_xor > 0.0, ranks[experts:], -1.0)
        slot = lax.broadcasted_iota(jnp.int32, (CAP, tok_count), 0).astype(jnp.float32)
        lane = lax.broadcasted_iota(jnp.int32, (CAP, LANES), 1)
        for k in range(experts):
            onehot = jnp.where(
                jnp.broadcast_to(rank_xor[k : k + 1], (CAP, tok_count)) == slot, 1.0, 0.0
            )
            onehot_ref[k * CAP : (k + 1) * CAP, :] = onehot.astype(jnp.bfloat16)
            slot_weight = jnp.sum(onehot * weight_xor[k : k + 1], axis=1, keepdims=True)
            row_refs[k][:, total:] = jnp.where(lane == 0, slot_weight, 0.0).astype(jnp.bfloat16)

    onehot = onehot_ref[...]
    cots = jnp.dot(onehot, cot_ref[...], preferred_element_type=jnp.float32).astype(jnp.bfloat16)
    toks = jnp.dot(onehot, tok_ref[...], preferred_element_type=jnp.float32).astype(jnp.bfloat16)
    start = pl.multiple_of(step * width, LANES)
    for k in range(experts):
        row_refs[k][:, pl.ds(start, width)] = cots[k * CAP : (k + 1) * CAP]
        row_refs[experts + k][:, pl.ds(start, width)] = toks[k * CAP : (k + 1) * CAP]


def pick_rows(me, ids, weight, tokens, cotangent, experts):
    tok_count, width = tokens.shape
    steps = 4
    block = width // steps
    whole = lambda shape: pl.BlockSpec(shape, lambda i: (0, 0))
    return pl.pallas_call(
        functools.partial(pick_kernel, experts, steps),
        grid=(steps,),
        in_specs=[
            pl.BlockSpec(memory_space=pltpu.SMEM),
            whole(ids.shape),
            whole(weight.shape),
            pl.BlockSpec((tok_count, block), lambda i: (0, i)),
            pl.BlockSpec((tok_count, block), lambda i: (0, i)),
        ],
        out_specs=[whole((CAP, width + LANES))] * experts
        + [whole((CAP, width))] * experts
        + [whole((experts, tok_count))],
        out_shape=[jax.ShapeDtypeStruct((CAP, width + LANES), jnp.bfloat16)] * experts
        + [jax.ShapeDtypeStruct((CAP, width), jnp.bfloat16)] * experts
        + [jax.ShapeDtypeStruct((experts, tok_count), jnp.float32)],
        scratch_shapes=[pltpu.VMEM((experts * CAP, tok_count), jnp.bfloat16)],
        name="pick_rows",
    )(me, ids, weight, tokens, cotangent)


def place_kernel(experts, ids_ref, rank_ref, sums_ref, out_ref):
    ids = ids_ref[...]
    rank = rank_ref[...]
    sums = jnp.sum(sums_ref[...], axis=1)
    value = jnp.zeros(rank.shape, jnp.float32)
    for slot in range(CAP):
        value = value + jnp.where(rank == float(slot), sums[:, slot : slot + 1], 0.0)
    grad = jnp.zeros(ids.shape, jnp.float32)
    for expert in range(experts):
        grad = grad + jnp.where(ids == expert, value[expert : expert + 1], 0.0)
    out_ref[...] = grad


def place_sums(ids, rank, sums, experts):
    return pl.pallas_call(
        functools.partial(place_kernel, experts),
        out_shape=jax.ShapeDtypeStruct(ids.shape, jnp.float32),
        name="place_sums",
    )(ids, rank, sums)


def line_gather(own, count):
    even = [(i, i + 1) for i in range(0, count - 1, 2)]
    odd = [(i, i + 1) for i in range(1, count - 1, 2)]
    swap = lambda pairs: pairs + [(b, a) for a, b in pairs]
    from_even, from_odd = own, own
    even_got, odd_got = [], []
    for step in range(count - 1):
        new_even = lax.ppermute(from_odd, "dp", swap(even))
        new_odd = lax.ppermute(from_even, "dp", swap(odd)) if step < count - 2 else None
        from_even, from_odd = new_even, new_odd
        even_got.append(new_even)
        odd_got.append(new_odd)
    return even_got, odd_got


def local(tokens, cotangent, route_ids, route_weight, gate_weight, up_weight, down_weight):
    expert_count = lax.axis_size("expert")
    dp_count = lax.axis_size("dp")
    if dp_count % 2 or expert_count & (expert_count - 1):
        raise ValueError("mesh size")
    tok_count, width = tokens.shape
    route_count = route_ids.shape[1]
    me = lax.axis_index("expert")
    at = lax.axis_index("dp")
    ids = route_ids.T
    rows = pick_rows(
        me[None].astype(jnp.int32), ids, route_weight.T, tokens, cotangent, expert_count
    )
    rank = rows[-1]
    cots, toks = rows[:expert_count], rows[expert_count:-1]

    def swap_expert(array, k):
        if k == 0:
            return array
        return lax.ppermute(array, "expert", [(i, i ^ k) for i in range(expert_count)])

    sign = jnp.where(at % 2 == 0, 1, -1)
    ahead = jnp.where(at % 2 == 0, dp_count - 1 - at, at)

    def gather(own):
        even_got, odd_got = line_gather(own, dp_count)
        parts = [own]
        for step in range(dp_count - 1):
            other = odd_got[dp_count - 2 - step]
            if other is None:
                parts.append(even_got[step])
            else:
                parts.append(jnp.where(step < ahead, even_got[step], other))
        return parts

    near = min(2, expert_count)
    cots = [swap_expert(c, k) for k, c in enumerate(cots)]
    toks = [swap_expert(t, k) for k, t in enumerate(toks)]
    cot_near = gather(jnp.concatenate(cots[:near], axis=0))
    cot_far = gather(jnp.concatenate(cots[near:], axis=0))
    tok_all = gather(jnp.concatenate(toks, axis=0))
    cot_block = jnp.concatenate([x for pair in zip(cot_near, cot_far) for x in pair], axis=0)
    row_block = jnp.concatenate(tok_all, axis=0)
    weights = cot_block[:, width : width + 1].astype(jnp.float32)
    w_gate, w_up, w_down = gate_weight[0], up_weight[0], down_weight[0]
    back_proj = lax.dot_general(
        cot_block[:, :width], w_down, (((1,), (1,)), ((), ())), preferred_element_type=jnp.float32
    )
    gate_pre = jnp.dot(row_block, w_gate, preferred_element_type=jnp.float32)
    up_pre = jnp.dot(row_block, w_up, preferred_element_type=jnp.float32)
    gate_sig = jax.nn.sigmoid(gate_pre)
    gate_act = gate_pre * gate_sig
    summed = jnp.sum(gate_act * up_pre * back_proj, axis=1)
    act_grad = weights * back_proj
    d_gate = (act_grad * up_pre * gate_sig * (1.0 + gate_pre * (1.0 - gate_sig))).astype(
        jnp.bfloat16
    )
    d_up = (act_grad * gate_act).astype(jnp.bfloat16)
    summed = summed.reshape(dp_count, expert_count, CAP)
    dest_expert = jnp.arange(expert_count)[:, None, None, None, None]
    dest_dp = jnp.arange(dp_count)[None, :, None, None, None]
    slot = jnp.arange(dp_count)[None, None, :, None, None]
    k = jnp.arange(expert_count)[None, None, None, :, None]
    here = ((dest_expert ^ me) == k) & (((dest_dp - at) * sign) % dp_count == slot)
    partial_value = jnp.sum(jnp.where(here, summed[None, None], 0.0), axis=(2, 3)).reshape(
        expert_count * dp_count, 1, CAP
    )
    returned = lax.all_to_all(
        partial_value, ("expert", "dp"), split_axis=0, concat_axis=0, tiled=True
    )
    grad_g = lax.dot_general(
        row_block, d_gate, (((0,), (0,)), ((), ())), preferred_element_type=jnp.float32
    )
    grad_u = lax.dot_general(
        row_block, d_up, (((0,), (0,)), ((), ())), preferred_element_type=jnp.float32
    )
    route_grad = place_sums(
        ids, rank, returned.reshape(expert_count, dp_count, CAP), expert_count
    )
    return (
        grad_g.astype(jnp.bfloat16)[None],
        grad_u.astype(jnp.bfloat16)[None],
        route_grad.T,
    )


def solution(mesh):
    return jax.shard_map(
        local,
        mesh=mesh,
        in_specs=(
            P(("groups", "expert", "dp"), None),
            P(("groups", "expert", "dp"), None),
            P(("groups", "expert", "dp"), None),
            P(("groups", "expert", "dp"), None),
            P("expert", None, "dp"),
            P("expert", None, "dp"),
            P("expert", "dp", None),
        ),
        out_specs=(
            P(("groups", "expert"), None, "dp"),
            P(("groups", "expert"), None, "dp"),
            P(("groups", "expert", "dp"), None),
        ),
        check_vma=False,
    )
```
